512 devices in a mesh: ctx: 64 (over x, z), head: 8 (over y, core).
Axes of the slice: x: 4, y: 4, z: 16, core: 2. Of those that a mesh axis runs over, the one named last changes fastest.
Arguments:
- query_rows: bfloat16 [8192, 6144], P('ctx', 'head'), may hold values from -6 to 6
- key_rows: bfloat16 [8192, 6144], P('ctx', 'head'), may hold values from -6 to 6
- value_rows: bfloat16 [8192, 6144], P('ctx', 'head'), may hold values from -6 to 6
- residual: bfloat16 [8192, 6144], P('ctx', 'head'), may hold values from -12 to 12
- attn_gain: float32 [6144], P('head'), may hold values from 0.5 to 1.5
- ffn_gain: float32 [6144], P('head'), may hold values from 0.5 to 1.5
- router_weight: bfloat16 [6144, 16], P('head'), may hold values from -0.078125 to 0.078125
- up_weight: bfloat16 [6144, 73728], P('head', 'ctx'), may hold values from -0.078125 to 0.078125
- down_weight: bfloat16 [73728, 6144], P('ctx', 'head'), may hold values from -0.09375 to 0.09375
- expert_ids: int32 [8192, 2], P('ctx'), may hold values from 0 to 15, as said below
Outputs:
- hidden: bfloat16 [8192, 6144], P('ctx', 'head')
- moe_out: bfloat16 [8192, 6144], P('ctx', 'head')
The draws below stay inside these ranges and needn't reach their ends.
Inputs may be any that keep to these rules, and one draw needn't show every extreme that they name: `expert_ids`: each row names two different experts. In the rows of one device (aligned blocks of 128 rows) one expert, the same for every block, is named exactly 24 times, and every other expert (232) // 15 times or once more.
All inputs are finite; a program needn't handle non-finite values.
Results may differ from the reference program's by a relative error of at most 0.025.
Values may be sent and summed in bfloat16 or wider, within the bound.
A program may use at most 128 MiB of HBM per device.

```python
import jax
import jax.numpy as jnp
from jax import lax

HEAD_DIM = 128
HEADS = 48
D = 6144
EXPERTS = 16
FF = 4608
TOK_DEV = 128
CAP = 24
GROUP = 4
TOKENS = 8192
N_CTX = 64
N_HEAD = 8


def draw_residual(key, part):
    first_key, second_key = jax.random.split(jax.random.fold_in(key, 11))
    column = jnp.arange(D, dtype=jnp.float32) / D
    rough = jax.random.uniform(first_key, (D,), minval=0.6, maxval=1.5)
    scale = 0.4 * jnp.exp(column * jnp.log(6.0)) * rough
    values = jax.random.normal(second_key, (TOKENS, D)) * scale
    return jnp.clip(values, -12.0, 12.0).astype(jnp.bfloat16)


def draw_expert_ids(key, part):
    label_key, block_key = jax.random.split(jax.random.fold_in(key, 23))
    relabel = jax.random.permutation(label_key, EXPERTS).astype(jnp.int32)
    block_total = TOKENS // TOK_DEV

    def one_block(this_key):
        start_key, flip_key, order_key = jax.random.split(this_key, 3)
        index = jnp.arange(2 * TOK_DEV, dtype=jnp.int32)
        offset = jax.random.randint(start_key, (), 0, EXPERTS - 1)
        other = 1 + (index - CAP + offset) % (EXPERTS - 1)
        labels = jnp.where(index < CAP, 0, other).astype(jnp.int32)
        paired = jnp.stack([labels[:TOK_DEV], labels[TOK_DEV:]], axis=1)
        flipped = jax.random.randint(flip_key, (TOK_DEV,), 0, 2)
        paired = jnp.where(flipped[:, None] == 1, paired[:, ::-1], paired)
        order = jax.random.permutation(order_key, TOK_DEV)
        return paired[order]
    keys = jax.random.split(block_key, block_total)
    chosen = jax.vmap(one_block)(keys).reshape(TOKENS, 2)
    return relabel[chosen].astype(jnp.int32)


def block_levels(rng, shape, cuts, least, high):
    gain, own = 1.0, jax.random.fold_in(rng, 6)
    for dim, blocks in cuts:
        steps = jnp.exp(jax.random.uniform(jax.random.fold_in(own, dim), (blocks,), jnp.float32, least / len(cuts), high / len(cuts)))
        gain = gain * jnp.repeat(steps, shape[dim] // blocks).reshape([-1 if axis == dim else 1 for axis in range(len(shape))])
    return gain


def scatter_about(stream_key, extent, width, most, cuts=(), held_as=jnp.bfloat16):
    result = width * jax.random.normal(stream_key, extent, jnp.float32)
    if cuts:
        result = result * block_levels(stream_key, extent, cuts, -0.22, 0.18)
    return jnp.clip(result, -most, most).astype(held_as)


def setup_inputs(seed: int = 0) -> dict:
    key_of = jax.random.split(jax.random.key(seed), 11)
    return {
        "query_rows": scatter_about(key_of[0], (TOKENS, D), 1.0, 6.0, ((0, 64), (1, 8))),
        "key_rows": scatter_about(key_of[1], (TOKENS, D), 1.0, 6.0, ((0, 64), (1, 8))),
        "value_rows": scatter_about(key_of[2], (TOKENS, D), 1.0, 6.0, ((0, 64), (1, 8))),
        "residual": draw_residual(jax.random.fold_in(key_of[10], 71), 0),
        "attn_gain": jnp.clip(1.0 + 0.1 * jax.random.normal(key_of[4], (D,), jnp.float32), 0.5, 1.5),
        "ffn_gain": jnp.clip(1.0 + 0.1 * jax.random.normal(key_of[5], (D,), jnp.float32), 0.5, 1.5),
        "router_weight": scatter_about(key_of[6], (D, EXPERTS), D ** -0.5, 0.078125, ((0, 8),)),
        "up_weight": scatter_about(key_of[7], (D, EXPERTS * FF), D ** -0.5, 0.078125, ((0, 8), (1, 64))),
        "down_weight": scatter_about(key_of[8], (EXPERTS * FF, D), FF ** -0.5, 0.09375, ((0, 64), (1, 8))),
        "expert_ids": draw_expert_ids(jax.random.fold_in(key_of[10], 71), 0),
    }


def attention_blocks(query_rows, key_rows, value_rows):

    def split_blocks(rows):
        return rows.reshape(N_CTX, TOK_DEV, HEADS, HEAD_DIM).transpose(0, 2, 1, 3)
    causal = jnp.arange(TOK_DEV)[:, None] >= jnp.arange(TOK_DEV)[None, :]

    def advance(state, blocks):
        query_blk, key_blk, value_blk = blocks
        query_f = query_blk.astype(jnp.float32)
        key_f = key_blk.astype(jnp.float32)
        value_f = value_blk.astype(jnp.float32)
        scores = jnp.einsum('htd,hsd->hts', query_f, key_f)
        scores = jnp.where(causal[None], scores, jnp.float32(0.0)).astype(jnp.bfloat16)
        local_part = jnp.einsum('hts,hsd->htd', scores.astype(jnp.float32), value_f)
        carried = jnp.einsum('htd,hde->hte', query_f, state, precision=lax.Precision.HIGHEST)
        new_state = state + jnp.einsum('hsd,hse->hde', key_f, value_f)
        return (new_state, local_part + carried)
    start = jnp.zeros((HEADS, HEAD_DIM, HEAD_DIM), jnp.float32)
    _, attn_raw = lax.scan(advance, start, (split_blocks(query_rows), split_blocks(key_rows), split_blocks(value_rows)))
    mean_sq = lax.optimization_barrier(jnp.mean(attn_raw * attn_raw, axis=-1, keepdims=True))
    normed = attn_raw * lax.rsqrt(mean_sq + 1e-05)
    return normed.transpose(0, 2, 1, 3).reshape(TOKENS, D)

def expert_layer(normed_rows, expert_ids, up_weight, down_weight):
    flat_ids = expert_ids.reshape(N_CTX, TOK_DEV * 2)
    flat_hot = (flat_ids[:, :, None] == jnp.arange(EXPERTS, dtype=jnp.int32)[None, None, :]).astype(jnp.int32)
    earlier = jnp.cumsum(flat_hot, axis=1) - flat_hot
    slot_rank = lax.optimization_barrier(jnp.sum(earlier * flat_hot, axis=-1)).astype(jnp.int32)
    source = jnp.arange(N_CTX, dtype=jnp.int32)[:, None]
    position = ((source * EXPERTS + flat_ids) * CAP + slot_rank).reshape(TOKENS * 2).astype(jnp.int32)
    token_of = jnp.arange(TOKENS * 2, dtype=jnp.int32) // 2
    buffer = jnp.zeros((N_CTX * EXPERTS * CAP, D), jnp.bfloat16).at[position].set(normed_rows[token_of])
    by_expert = buffer.reshape(N_CTX, EXPERTS, CAP, D).transpose(1, 0, 2, 3).reshape(EXPERTS, N_CTX * CAP, D)

    def run_expert(inputs):
        row_block, expert_idx = inputs
        start = (expert_idx * FF).astype(jnp.int32)
        w_up = lax.dynamic_slice_in_dim(up_weight, start, FF, 1)
        w_down = lax.dynamic_slice_in_dim(down_weight, start, FF, 0)
        row_count = row_block.shape[0]
        pieces = jnp.einsum('rhd,hdf->rhf', row_block.reshape(row_count, N_HEAD, D // N_HEAD).astype(jnp.float32), w_up.reshape(N_HEAD, D // N_HEAD, FF).astype(jnp.float32))
        pre = lax.optimization_barrier(jnp.sum(pieces.astype(jnp.bfloat16).astype(jnp.float32), axis=1))
        active = jax.nn.silu(pre).astype(jnp.bfloat16)
        parts = jnp.einsum('rgf,gfd->rgd', active.reshape(row_count, GROUP, FF // GROUP).astype(jnp.float32), w_down.reshape(GROUP, FF // GROUP, D).astype(jnp.float32))
        return lax.optimization_barrier(jnp.sum(parts.astype(jnp.bfloat16).astype(jnp.float32), axis=1))
    expert_out = lax.map(run_expert, (by_expert, jnp.arange(EXPERTS, dtype=jnp.int32)))
    flat_out = expert_out.reshape(EXPERTS, N_CTX, CAP, D).transpose(1, 0, 2, 3).reshape(N_CTX * EXPERTS * CAP, D)
    return flat_out[position].reshape(TOKENS, 2, D)

def reference(query_rows, key_rows, value_rows, residual, attn_gain, ffn_gain, router_weight, up_weight, down_weight, expert_ids):
    attn = attention_blocks(query_rows, key_rows, value_rows)
    hidden = (residual.astype(jnp.float32) + attn_gain * attn).astype(jnp.bfloat16)
    hidden_f = hidden.astype(jnp.float32)
    inv_rms = lax.rsqrt(lax.optimization_barrier(jnp.mean(hidden_f * hidden_f, axis=-1, keepdims=True)) + 1e-05)
    scaled = hidden_f * ffn_gain
    normed = (scaled * inv_rms).astype(jnp.bfloat16)
    logits = jnp.dot(scaled, router_weight.astype(jnp.float32), precision=lax.Precision.HIGHEST) * inv_rms
    picked = jnp.take_along_axis(logits, expert_ids, axis=1)
    first = jax.nn.sigmoid(picked[:, 0] - picked[:, 1])
    gates = jnp.stack([first, 1.0 - first], axis=1)
    routed = expert_layer(normed, expert_ids, up_weight, down_weight)
    moe_out = lax.optimization_barrier(jnp.sum(gates[:, :, None] * routed, axis=1)).astype(jnp.bfloat16)
    return (hidden, moe_out)
```

```python
import jax
import jax.numpy as jnp
from jax import lax
from jax.experimental import pallas as pl
from jax.experimental.pallas import tpu as pltpu
from jax.sharding import PartitionSpec as P

HEAD_DIM = 128
D = 6144
EXPERTS = 16
CAP = 24
NX = 4
NZ = 16
NY = 4
MESH = pl.DeviceIdType.MESH
F32 = jnp.float32
BF16 = jnp.bfloat16
HIGHEST = lax.Precision.HIGHEST


def spot():
    ctx = lax.axis_index("ctx")
    head = lax.axis_index("head")
    return ctx // NZ, ctx % NZ, head // 2, head % 2


def send(src, dst, send_sem, recv_sem, ctx, head):
    copy = pltpu.make_async_remote_copy(
        src_ref=src,
        dst_ref=dst,
        send_sem=send_sem,
        recv_sem=recv_sem,
        device_id=(ctx, head),
        device_id_type=MESH,
    )
    copy.start()
    return copy


def await_bytes(ref, sem):
    pltpu.make_async_copy(ref, ref, sem).wait()


def greet(barrier, ctx, head):
    pl.semaphore_signal(barrier, inc=1, device_id=(ctx, head), device_id_type=MESH)


def dot(a, b, dims, precision=None):
    return lax.dot_general(a, b, (dims, ((), ())), precision=precision, preferred_element_type=F32)


def attend(
    ids_ref,
    query_ref,
    key_ref,
    value_ref,
    residual_ref,
    attn_gain_ref,
    ffn_gain_ref,
    router_ref,
    up_ref,
    down_ref,
    hidden_ref,
    outgoing_ref,
    meta_ref,
    up_other_ref,
    down_other_ref,
    state,
    landed,
    total,
    totals,
    before,
    answer,
    prior,
    local,
    stats,
    all_stats,
    weight_send,
    weight_recv,
    state_send,
    state_recv,
    total_send,
    total_recv,
    answer_send,
    answer_recv,
    stat_send,
    stat_recv,
):
    x, z, y, core = spot()
    ctx = x * NZ + z
    head = y * 2 + core
    heads = query_ref.shape[1] // HEAD_DIM
    rows = query_ref.shape[0]
    part = heads * HEAD_DIM // NZ

    barrier = pltpu.get_barrier_semaphore()
    for dz in range(1, NZ):
        greet(barrier, x * NZ + (z + dz) % NZ, head)
    for dx in range(1, NX):
        greet(barrier, ((x + dx) % NX) * NZ + z, head)
    for dh in range(1, 8):
        greet(barrier, ctx, (head + dh) % 8)

    for h in range(heads):
        cols = slice(h * HEAD_DIM, (h + 1) * HEAD_DIM)
        state[cols, :] = dot(key_ref[:, cols], value_ref[:, cols], ((0,), (0,))).astype(BF16)

    pl.semaphore_wait(barrier, 25)

    def slab(index):
        return pl.ds(pl.multiple_of(index * part, 16), part)

    state_copies = []
    for dz in range(1, NZ):
        other = (z + dz) % NZ
        state_copies.append(
            send(state.at[slab(other)], landed.at[z], state_send, state_recv, x * NZ + other, head)
        )
    mate = y * 2 + 1 - core
    up_copy = send(up_ref, up_other_ref, weight_send.at[0], weight_recv.at[0], ctx, mate)
    down_copy = send(down_ref, down_other_ref, weight_send.at[1], weight_recv.at[1], ctx, mate)

    landed[z] = state[slab(z), :]
    row_iota = lax.broadcasted_iota(jnp.int32, (rows, rows), 0)
    col_iota = lax.broadcasted_iota(jnp.int32, (rows, rows), 1)
    for h in range(heads):
        cols = slice(h * HEAD_DIM, (h + 1) * HEAD_DIM)
        scores = dot(query_ref[:, cols], key_ref[:, cols], ((1,), (1,)))
        scores = jnp.where(row_iota >= col_iota, scores, 0.0).astype(BF16)
        local[:, cols] = dot(scores, value_ref[:, cols], ((1,), (0,)))

    await_bytes(landed.at[pl.ds(0, NZ - 1)], state_recv)
    running = jnp.zeros((part, HEAD_DIM), F32)
    for turn in range(NZ):
        before[turn] = running
        running = running + landed[turn].astype(F32)
    total[...] = running
    for dx in range(1, NX):
        other = (x + dx) % NX
        send(total, totals.at[x], total_send, total_recv, other * NZ + z, head)
    await_bytes(totals.at[pl.ds(0, NX - 1)], total_recv)
    base = jnp.zeros((part, HEAD_DIM), F32)
    for turn in range(NX - 1):
        base = base + jnp.where(turn < x, totals[turn], 0.0)
    for turn in range(NZ):
        answer[turn] = (before[turn] + base).astype(BF16)
    for dz in range(1, NZ):
        other = (z + dz) % NZ
        send(answer.at[other], prior.at[slab(z)], answer_send, answer_recv, x * NZ + other, head)
    prior[slab(z), :] = answer[z]

    eye = row_iota == col_iota
    ids = ids_ref[...]
    row_ids = [
        jnp.sum(jnp.where(eye, ids[:, k : k + 1], 0), axis=0, keepdims=True) for k in range(2)
    ]
    expert_iota = lax.broadcasted_iota(jnp.int32, (EXPERTS, rows), 0)
    hots = [expert_iota == row for row in row_ids]
    both = (hots[0] | hots[1]).astype(F32).astype(BF16)
    strict = (row_iota < col_iota).astype(F32).astype(BF16)
    counts = dot(both, strict, ((1,), (0,)))
    places = [
        row.astype(F32) * CAP + jnp.sum(jnp.where(hot, counts, 0.0), axis=0, keepdims=True)
        for row, hot in zip(row_ids, hots)
    ]

    await_bytes(answer.at[pl.ds(0, NZ - 1)], answer_recv)
    for h in range(heads):
        cols = slice(h * HEAD_DIM, (h + 1) * HEAD_DIM)
        raw = local[:, cols] + dot(query_ref[:, cols], prior[cols, :], ((1,), (0,)))
        mean_sq = jnp.mean(raw * raw, axis=-1, keepdims=True)
        normal = raw * lax.rsqrt(mean_sq + 1e-05)
        hidden_ref[:, cols] = (
            residual_ref[:, cols].astype(F32) + attn_gain_ref[:, cols] * normal
        ).astype(BF16)
    hidden = hidden_ref[...].astype(F32)
    scaled = hidden * ffn_gain_ref[...]
    ones = jnp.ones((8, hidden.shape[1]), F32)
    stats[0:EXPERTS, :] = dot(router_ref[...].astype(F32), scaled, ((1,), (1,)), HIGHEST)
    stats[EXPERTS : EXPERTS + 8, :] = dot(ones, hidden * hidden, ((1,), (1,)), HIGHEST)
    for dh in range(1, 8):
        send(stats, all_stats.at[head], stat_send, stat_recv, ctx, (head + dh) % 8)
    all_stats[head] = stats[...]
    await_bytes(all_stats.at[pl.ds(0, 7)], stat_recv)
    summed = all_stats[0]
    for turn in range(1, 8):
        summed = summed + all_stats[turn]
    inv_row = lax.rsqrt(summed[EXPERTS : EXPERTS + 1, :] / D + 1e-05)
    logits = summed[0:EXPERTS, :] * inv_row
    picked = [jnp.sum(jnp.where(hot, logits, 0.0), axis=0, keepdims=True) for hot in hots]
    first = jax.nn.sigmoid(picked[0] - picked[1])
    meta_ref[...] = jnp.concatenate(
        [places[0], places[1], first, 1.0 - first, jnp.zeros((4, rows), F32)], axis=0
    )
    inv_col = jnp.sum(jnp.where(eye, inv_row, 0.0), axis=1, keepdims=True)
    normed = (scaled * inv_col).astype(BF16)
    slot_iota = lax.broadcasted_iota(jnp.int32, (EXPERTS * CAP, rows), 0).astype(F32)
    table = ((slot_iota == places[0]) | (slot_iota == places[1])).astype(F32).astype(BF16)
    outgoing_ref[...] = dot(table, normed, ((1,), (0,))).astype(BF16)

    await_bytes(landed.at[pl.ds(0, NZ - 1)], state_send)
    await_bytes(totals.at[pl.ds(0, NX - 1)], total_send)
    await_bytes(answer.at[pl.ds(0, NZ - 1)], answer_send)
    await_bytes(all_stats.at[pl.ds(0, 7)], stat_send)
    up_copy.wait()
    down_copy.wait()


def run_attend(ids, query, key, value, residual, attn_gain, ffn_gain, router, up, down):
    rows, width = query.shape
    part = width // NZ
    vmem = pl.BlockSpec(memory_space=pltpu.VMEM)
    anywhere = pl.BlockSpec(memory_space=pl.ANY)
    dma = pltpu.SemaphoreType.DMA
    return pl.pallas_call(
        attend,
        out_shape=(
            jax.ShapeDtypeStruct((rows, width), BF16),
            jax.ShapeDtypeStruct((EXPERTS * CAP, width), BF16),
            jax.ShapeDtypeStruct((8, rows), F32),
            jax.ShapeDtypeStruct(up.shape, BF16),
            jax.ShapeDtypeStruct(down.shape, BF16),
        ),
        in_specs=[vmem] * 8 + [anywhere] * 2,
        out_specs=(vmem, vmem, vmem, anywhere, anywhere),
        scratch_shapes=[
            pltpu.VMEM((width, HEAD_DIM), BF16),
            pltpu.VMEM((NZ, part, HEAD_DIM), BF16),
            pltpu.VMEM((part, HEAD_DIM), F32),
            pltpu.VMEM((NX, part, HEAD_DIM), F32),
            pltpu.VMEM((NZ, part, HEAD_DIM), F32),
            pltpu.VMEM((NZ, part, HEAD_DIM), BF16),
            pltpu.VMEM((width, HEAD_DIM), BF16),
            pltpu.VMEM((rows, width), F32),
            pltpu.VMEM((EXPERTS + 8, rows), F32),
            pltpu.VMEM((8, EXPERTS + 8, rows), F32),
            dma((2,)),
            dma((2,)),
            dma,
            dma,
            dma,
            dma,
            dma,
            dma,
            dma,
            dma,
        ],
        compiler_params=pltpu.CompilerParams(
            collective_id=0, has_side_effects=True, vmem_limit_bytes=48 * 1024 * 1024
        ),
        name="attend",
    )(ids, query, key, value, residual, attn_gain, ffn_gain, router, up, down)


def body(
    query_rows,
    key_rows,
    value_rows,
    residual,
    attn_gain,
    ffn_gain,
    router_weight,
    up_weight,
    down_weight,
    expert_ids,
):
    tok_rows, feat_width = query_rows.shape
    hidden, outgoing, meta, up_other, down_other = run_attend(
        expert_ids,
        query_rows,
        key_rows,
        value_rows,
        residual,
        attn_gain[None, :],
        ffn_gain[None, :],
        router_weight.T,
        up_weight,
        down_weight,
    )
    slot_iota = jnp.arange(EXPERTS * CAP, dtype=jnp.int32).astype(F32)[None, :]
    combine_table = jnp.where(slot_iota == meta[0][:, None], meta[2][:, None], 0.0) + jnp.where(
        slot_iota == meta[1][:, None], meta[3][:, None], 0.0
    )
    group_size = lax.axis_size("ctx") // EXPERTS
    outgoing = jnp.repeat(outgoing.reshape(EXPERTS, CAP, feat_width), group_size, axis=0)
    arrived = lax.all_to_all(outgoing, "ctx", split_axis=0, concat_axis=0, tiled=True)
    sources, slot_count, width_in = arrived.shape
    row_block = arrived.reshape(sources * slot_count, width_in)
    partial_value = jnp.dot(row_block, up_weight, preferred_element_type=jnp.float32)
    active = jax.nn.silu(
        lax.psum(partial_value.astype(jnp.bfloat16), "head").astype(jnp.float32)
    ).astype(jnp.bfloat16)
    part_out = jnp.dot(active, down_weight, preferred_element_type=jnp.float32).astype(jnp.bfloat16)
    expert_parts = part_out.reshape(sources, slot_count, width_in)
    returned = lax.all_to_all(expert_parts, "ctx", split_axis=0, concat_axis=0, tiled=True)
    expert_out = jnp.sum(
        returned.reshape(EXPERTS, group_size, CAP, feat_width).astype(jnp.float32), axis=1
    )
    expert_out = expert_out.reshape(EXPERTS * CAP, feat_width)
    moe_out = jnp.dot(combine_table, expert_out, precision=lax.Precision.HIGHEST).astype(
        jnp.bfloat16
    )
    return (hidden, moe_out)


def solution(mesh):
    placed = (
        P("ctx", "head"),
        P("ctx", "head"),
        P("ctx", "head"),
        P("ctx", "head"),
        P("head"),
        P("head"),
        P("head", None),
        P("head", "ctx"),
        P("ctx", "head"),
        P("ctx", None),
    )
    return jax.shard_map(
        body,
        mesh=mesh,
        in_specs=placed,
        out_specs=(P("ctx", "head"), P("ctx", "head")),
        check_vma=False,
    )
```
